128 devices in a mesh: row: 16 (over z, y_hi, core), col: 8 (over y_lo, x).
Axes of the slice: x: 4, y: 4 (y_hi: 2, y_lo: 2; y = y_hi * 2 + y_lo), z: 4, core: 2. Of those that a mesh axis runs over, the one named last changes fastest.
Arguments:
- packed_tiles: bfloat16 [768, 128, 1024], P('row', None, 'col'), may hold values from -6 to 6
- source_pick: int32 [16, 48], P('row'), may hold values from 0 to 47, each once within a row
- owner_place: int32 [16, 48], P('row'), may hold values from 0 to 47, each once within a row
- tile_orient: int32 [16, 48], P('row'), may hold values from 0 to 3
- w_panel: bfloat16 [4096, 12288], P('row', 'col'), may hold values from -0.09375 to 0.09375
Outputs:
- particle_hole: bfloat16 [24576, 12288], P('row', 'col')
The draws below stay inside these ranges and needn't reach their ends.
Inputs may be any that keep to these rules, and one draw needn't show every extreme that they name: `source_pick`: each row is a permutation of the stored tiles' local indices. `owner_place`: each row is a permutation of the received items.
All inputs are finite; a program needn't handle non-finite values.
Results may differ from the reference program's by a relative error of at most 0.001.
Values may be sent and summed in bfloat16 or wider, within the bound.
No kernel may reach another device: no remote copies, remote signals or barrier semaphores. Data moves between devices by JAX's collectives and lax.ppermute only.
A program may use at most 128 MiB of HBM per device.

```python
import jax
import jax.numpy as jnp

TILE = 128
VW = 768
KC = 512
STORED = 48
ROWS = 24576
COLS = 12288
K = 4096
N_ROW = 16
N_COL = 8


def with_ends(values, key, low, top_value):
    place = [jax.random.randint(jax.random.fold_in(key, axis), (), 0, length) for axis, length in enumerate(values.shape)]
    main_axis = values.shape.index(max(values.shape))
    beside = place[:main_axis] + [(place[main_axis] + 1) % values.shape[main_axis]] + place[main_axis + 1:]
    return values.at[tuple(place)].set(low).at[tuple(beside)].set(top_value)


def level_of(rng, shape, split, smallest, largest):
    def one(dim, shards_of):
        heights = jax.random.uniform(jax.random.fold_in(jax.random.fold_in(rng, 6), dim), (shards_of,), jnp.float32, smallest / len(split), largest / len(split))
        return jnp.repeat(jnp.exp(heights), shape[dim] // shards_of).reshape((-1,) + (1,) * (len(shape) - dim - 1))

    gain = one(*split[0])
    for cut in split[1:]:
        gain = gain * one(*cut)
    return gain


def gaussian(key, extent, spread, limit, shards=(), held_as=jnp.bfloat16):
    entries = jax.random.normal(key, extent, jnp.float32) * spread
    if len(shards) > 0:
        entries = level_of(key, extent, shards, -0.22, 0.18) * entries
    return jnp.clip(entries, min=-limit, max=limit).astype(held_as)


def setup_inputs(seed: int = 0) -> dict:
    splits = jax.random.split(jax.random.key(seed), 6)
    return {
        "packed_tiles": gaussian(splits[0], (N_ROW * STORED, TILE, N_COL * TILE), 1.0, 6.0, ((0, 16), (2, 8))),
        "source_pick": jax.vmap(lambda own: jax.random.permutation(own, STORED))(jax.random.split(splits[1], N_ROW)).reshape((N_ROW, STORED)).astype(jnp.int32),
        "owner_place": jax.vmap(lambda own: jax.random.permutation(own, STORED))(jax.random.split(splits[2], N_ROW)).reshape((N_ROW, STORED)).astype(jnp.int32),
        "tile_orient": with_ends(jax.random.randint(splits[3], (N_ROW, STORED), 0, 4), jax.random.fold_in(splits[3], 1), 0, 3).astype(jnp.int32),
        "w_panel": gaussian(splits[4], (K, COLS), K ** -0.5, 0.09375, ((0, 16), (1, 8))),
    }


def reference(packed_tiles, source_pick, owner_place, tile_orient, w_panel):
    peer_slots = STORED // N_ROW
    target = jnp.arange(N_ROW, dtype=jnp.int32)[:, None]
    source = owner_place // peer_slots
    slot_index = owner_place % peer_slots
    local_index = source_pick[source, target * peer_slots + slot_index]
    flat_index = (source * STORED + local_index).reshape(-1).astype(jnp.int32)
    tile_set = packed_tiles[flat_index].reshape(N_ROW * STORED, TILE, N_COL, TILE)
    orient_codes = tile_orient.reshape(-1)
    flipped = (orient_codes % 2 == 1)[:, None, None, None]
    negated = (orient_codes >= 2)[:, None, None, None]
    turned = jnp.where(flipped, jnp.swapaxes(tile_set, 1, 3), tile_set)
    turned = jnp.where(negated, -turned, turned)
    col_tiles = KC // TILE
    row_tiles = STORED // col_tiles
    lambda_rows = turned.reshape(N_ROW, row_tiles, col_tiles, TILE, N_COL, TILE)
    lambda_rows = lambda_rows.transpose(0, 1, 3, 4, 2, 5).reshape(ROWS, K)
    product = jnp.dot(lambda_rows, w_panel, preferred_element_type=jnp.float32)
    blocked = product.reshape(ROWS // VW, VW, COLS // VW, VW)
    return (blocked - blocked.transpose(0, 3, 2, 1)).reshape(ROWS, COLS).astype(jnp.bfloat16)
```

```python
import functools

import jax
import jax.numpy as jnp
from jax import lax
from jax.experimental import pallas as pl
from jax.experimental.pallas import tpu as pltpu
from jax.sharding import PartitionSpec as P

TILE = 128
VW = 768
KC = 512
STORED = 48
COL_TILES = KC // TILE
ROW_TILES = STORED // COL_TILES
HALF_TILES = VW // TILE
NZ, NY, NX, NCORE = 4, 2, 4, 2
PANEL = 256
BREADTH = 1536
BF16, F32 = jnp.bfloat16, jnp.float32
VMEM_LIMIT = 60 << 20


def col_index(y_lo, x):
    return y_lo * NX + x


def row_index(z, y_hi, core):
    return (z * NY + y_hi) * NCORE + core


def col_move(dy, dx):
    return [
        (col_index(y, x), col_index(y ^ dy, (x + dx) % NX))
        for y in range(2)
        for x in range(NX)
    ]


def row_move(dz, dy, dc):
    return [
        (row_index(z, y, c), row_index((z + dz) % NZ, y ^ dy, c ^ dc))
        for z in range(NZ)
        for y in range(NY)
        for c in range(NCORE)
    ]


def pick_kernel(pick_ref, tiles_ref, out_ref, sem):
    def start(t, _):
        pltpu.make_async_copy(tiles_ref.at[pick_ref[0, t]], out_ref.at[t], sem).start()
        return 0

    lax.fori_loop(0, STORED, start, 0)
    pltpu.make_async_copy(tiles_ref, out_ref, sem).wait()


def pick_tiles(packed_tiles, source_pick):
    return pl.pallas_call(
        pick_kernel,
        out_shape=jax.ShapeDtypeStruct(packed_tiles.shape, BF16),
        in_specs=[
            pl.BlockSpec(memory_space=pltpu.SMEM),
            pl.BlockSpec(memory_space=pl.ANY),
        ],
        out_specs=pl.BlockSpec(memory_space=pltpu.VMEM),
        scratch_shapes=[pltpu.SemaphoreType.DMA],
        compiler_params=pltpu.CompilerParams(vmem_limit_bytes=VMEM_LIMIT),
        cost_estimate=pl.CostEstimate(
            flops=0, bytes_accessed=4 * packed_tiles.size, transcendentals=0
        ),
        name="pick_tiles",
    )(source_pick, packed_tiles)


def orient_kernel(place_ref, orient_ref, tiles_ref, top_ref, bottom_ref):
    for half, out_ref in enumerate((top_ref, bottom_ref)):

        def body(k, _):
            o = half * HALF_TILES * COL_TILES + k
            code = orient_ref[0, o]
            tile = tiles_ref[place_ref[0, o]]
            signed = jnp.where(code >= 2, -tile, tile)
            rows = pl.ds(pl.multiple_of(k // COL_TILES * TILE, TILE), TILE)
            cols = pl.ds(pl.multiple_of(k % COL_TILES * TILE, TILE), TILE)

            @pl.when(code % 2 == 1)
            def _():
                out_ref[rows, cols] = signed.T

            @pl.when(code % 2 == 0)
            def _():
                out_ref[rows, cols] = signed

            return 0

        lax.fori_loop(0, HALF_TILES * COL_TILES, body, 0)


def orient_tiles(incoming, owner_place, tile_orient):
    half = jax.ShapeDtypeStruct((VW, KC), BF16)
    return pl.pallas_call(
        orient_kernel,
        out_shape=(half, half),
        in_specs=[
            pl.BlockSpec(memory_space=pltpu.SMEM),
            pl.BlockSpec(memory_space=pltpu.SMEM),
            pl.BlockSpec(memory_space=pltpu.VMEM),
        ],
        out_specs=(
            pl.BlockSpec(memory_space=pltpu.VMEM),
            pl.BlockSpec(memory_space=pltpu.VMEM),
        ),
        compiler_params=pltpu.CompilerParams(vmem_limit_bytes=VMEM_LIMIT),
        cost_estimate=pl.CostEstimate(
            flops=0, bytes_accessed=4 * incoming.size, transcendentals=0
        ),
        name="orient_tiles",
    )(owner_place, tile_orient, incoming)


def fetch(lefts, panels, chunks, lhs, rhs, sems):
    r, c = lax.axis_index("row"), lax.axis_index("col")
    z, y_hi, core = r // (NY * NCORE), r // NCORE % NY, r % NCORE
    y_lo, x = c // NX, c % NX
    for n, (dy, dx) in enumerate(chunks):
        pltpu.make_async_copy(
            lefts[n], lhs.at[:, pl.ds(n * KC, KC)], sems.at[0]
        ).start()
        g = (y_lo ^ dy) * NX + (x + dx) % NX
        which = (g // NY - z + NZ) % NZ * NY + (g % NY ^ y_hi)
        for k in range(NZ * NY):

            @pl.when(which == k)
            def _():
                for dc in range(NCORE):
                    at = n * KC + (core ^ dc) * PANEL
                    pltpu.make_async_copy(
                        panels[k * NCORE + dc],
                        rhs.at[pl.ds(pl.multiple_of(at, PANEL), PANEL)],
                        sems.at[1],
                    ).start()


def partial_kernel(chunks, *refs):
    n = len(chunks)
    lefts, panels = refs[:n], refs[n : n + 16]
    out_ref, lhs, rhs, sems = refs[n + 16 :]
    fetch(lefts, panels, chunks, lhs, rhs, sems)
    pltpu.make_async_copy(lhs, lhs, sems.at[0]).wait()
    pltpu.make_async_copy(rhs, rhs, sems.at[1]).wait()
    step = 256

    def body(j, _):
        cols = pl.ds(pl.multiple_of(j * step, step), step)
        out_ref[:, cols] = jnp.dot(
            lhs[...], rhs[:, cols], preferred_element_type=F32
        )
        return 0

    lax.fori_loop(0, BREADTH // step, body, 0)


def partial_product(chunks, lefts, panels, name):
    depth = len(chunks) * KC
    return pl.pallas_call(
        functools.partial(partial_kernel, chunks),
        out_shape=jax.ShapeDtypeStruct((VW, BREADTH), F32),
        in_specs=[pl.BlockSpec(memory_space=pl.ANY)] * (len(chunks) + 16),
        out_specs=pl.BlockSpec(memory_space=pltpu.VMEM),
        scratch_shapes=[
            pltpu.VMEM((VW, depth), BF16),
            pltpu.VMEM((depth, BREADTH), BF16),
            pltpu.SemaphoreType.DMA((2,)),
        ],
        compiler_params=pltpu.CompilerParams(vmem_limit_bytes=VMEM_LIMIT),
        cost_estimate=pl.CostEstimate(
            flops=2 * VW * depth * BREADTH,
            bytes_accessed=2 * depth * (VW + BREADTH) + 4 * VW * BREADTH,
            transcendentals=0,
        ),
        name=name,
    )(*lefts, *panels)


def final_kernel(chunks, half, aliased, *refs):
    n = len(chunks)
    lefts, panels, part = refs[:n], refs[n : n + 16], refs[n + 16]
    out_ref, lhs, rhs, total, res, sems = refs[n + 17 + aliased :]
    fetch(lefts, panels, chunks, lhs, rhs, sems)
    pltpu.make_async_copy(part, total, sems.at[2]).start()
    pltpu.make_async_copy(lhs, lhs, sems.at[0]).wait()
    pltpu.make_async_copy(rhs, rhs, sems.at[1]).wait()
    pltpu.make_async_copy(part, total, sems.at[2]).wait()
    step = 256

    def body(j, _):
        cols = pl.ds(pl.multiple_of(j * step, step), step)
        total[:, cols] += jnp.dot(lhs[...], rhs[:, cols], preferred_element_type=F32)
        return 0

    lax.fori_loop(0, BREADTH // step, body, 0)

    def turn(j, _):
        base = j * VW
        for a in range(HALF_TILES):
            for b in range(a, HALF_TILES):
                rows_a = pl.ds(a * TILE, TILE)
                rows_b = pl.ds(b * TILE, TILE)
                cols_a = pl.ds(pl.multiple_of(base + a * TILE, TILE), TILE)
                cols_b = pl.ds(pl.multiple_of(base + b * TILE, TILE), TILE)
                upper = total[rows_a, cols_b]
                lower = total[rows_b, cols_a]
                res[rows_a, cols_b] = (upper - lower.T).astype(BF16)
                if a != b:
                    res[rows_b, cols_a] = (lower - upper.T).astype(BF16)
        return 0

    lax.fori_loop(0, BREADTH // VW, turn, 0)
    copy = pltpu.make_async_copy(res, out_ref.at[pl.ds(half * VW, VW)], sems.at[3])
    copy.start()
    copy.wait()


def final_product(chunks, half, lefts, panels, part, out, name):
    depth = len(chunks) * KC
    aliased = int(out is not None)
    operands = [*lefts, *panels, part] + ([out] if aliased else [])
    return pl.pallas_call(
        functools.partial(final_kernel, chunks, half, aliased),
        out_shape=jax.ShapeDtypeStruct((2 * VW, BREADTH), BF16),
        in_specs=[pl.BlockSpec(memory_space=pl.ANY)] * len(operands),
        out_specs=pl.BlockSpec(memory_space=pl.ANY),
        scratch_shapes=[
            pltpu.VMEM((VW, depth), BF16),
            pltpu.VMEM((depth, BREADTH), BF16),
            pltpu.VMEM((VW, BREADTH), F32),
            pltpu.VMEM((VW, BREADTH), BF16),
            pltpu.SemaphoreType.DMA((4,)),
        ],
        input_output_aliases={len(operands) - 1: 0} if aliased else {},
        compiler_params=pltpu.CompilerParams(vmem_limit_bytes=VMEM_LIMIT),
        cost_estimate=pl.CostEstimate(
            flops=2 * VW * depth * BREADTH,
            bytes_accessed=2 * depth * (VW + BREADTH) + 6 * VW * BREADTH,
            transcendentals=0,
        ),
        name=name,
    )(*operands)


def gather_panel(w):
    send = lambda v, dz, dy, dc: lax.ppermute(v, "row", row_move(dz, dy, dc))
    got = {(0, 0): w}
    got[0, 1] = send(w, 0, 1, 0)
    for dy in range(NY):
        got[3, dy] = send(got[0, dy], 1, 0, 0)
        got[1, dy] = send(got[0, dy], -1, 0, 0)
    got[2, 0] = send(got[3, 0], 1, 0, 0)
    got[2, 1] = send(got[1, 1], -1, 0, 0)
    panels = []
    for dz in range(NZ):
        for dy in range(NY):
            panels += [got[dz, dy], send(got[dz, dy], 0, 0, 1)]
    return panels


def on_device(packed_tiles, source_pick, owner_place, tile_orient, w_panel):
    panels = gather_panel(w_panel)
    outgoing = pick_tiles(packed_tiles, source_pick)
    incoming = lax.all_to_all(
        outgoing.reshape(16, 3, TILE, TILE), "row", split_axis=0, concat_axis=0, tiled=True
    ).reshape(STORED, TILE, TILE)
    own = orient_tiles(incoming, owner_place, tile_orient)

    send = lambda v, dy, dx: lax.ppermute(v, "col", col_move(dy, dx))
    got = [{(0, 0): own[0]}, {(0, 0): own[1]}]
    for h in range(2):
        got[h][0, 3] = send(own[h], 0, 1)
        got[h][0, 1] = send(own[h], 0, -1)
        got[h][1, 0] = send(own[h], 1, 0)
    got[0][0, 2] = send(got[0][0, 3], 0, 1)
    got[1][0, 2] = send(got[1][0, 1], 0, -1)
    for h in range(2):
        got[h][1, 3] = send(got[h][1, 0], 0, 1)
        got[h][1, 1] = send(got[h][1, 0], 0, -1)
        got[h][1, 2] = send(got[h][0, 2], 1, 0)

    early = ((0, 0), (0, 1), (0, 3), (1, 0), (0, 2))
    late = ((1, 1), (1, 3), (1, 2))
    parts = [
        partial_product(early, [got[h][k] for k in early], panels, f"early_{h}")
        for h in range(2)
    ]
    out = None
    for h in range(2):
        out = final_product(
            late, h, [got[h][k] for k in late], panels, parts[h], out, f"late_{h}"
        )
    return out


def solution(mesh):
    in_specs = (
        P("row", None, "col"),
        P("row", None),
        P("row", None),
        P("row", None),
        P("row", "col"),
    )
    out_specs = P("row", "col")
    return jax.shard_map(
        on_device, mesh=mesh, in_specs=in_specs, out_specs=out_specs, check_vma=False
    )
```
